128 devices in a mesh: row: 8 (over z, core), col: 16 (over y, x).
Axes of the slice: x: 4, y: 4, z: 4, core: 2. Of those that a mesh axis runs over, the one named last changes fastest.
Arguments:
- initial: bfloat16 [8, 24576], P(None, ('row', 'col')), may hold values from -8 to 8
- matrix: bfloat16 [24576, 24576], P('row', 'col'), may hold values from -1 to 4, as said below
Outputs:
- vectors: float32 [8, 24576], P(None, ('row', 'col'))
- estimates: float32 [4, 8], replicated
The draws below stay inside these ranges and needn't reach their ends.
Inputs may be any that keep to these rules, and one draw needn't show every extreme that they name: matrix is symmetric: entry (i, j) equals entry (j, i).
All inputs are finite; a program needn't handle non-finite values.
Results may differ from the reference program's by a relative error of at most 0.008.
Values may be sent and summed in bfloat16 or wider, within the bound.
No kernel may reach another device: no remote copies, remote signals or barrier semaphores. Data moves between devices by JAX's collectives and lax.ppermute only.
A program may use at most 64 MiB of HBM per device.

```python
import math
import jax
import jax.numpy as jnp
from jax import lax

N = 24576
K = 8
ITERS = 4


def draw_initial(key, part):
    shared = jnp.clip(jax.random.normal(jax.random.fold_in(key, 11), (N,), jnp.float32), -3.0, 3.0)
    signs = jnp.where(jax.random.bernoulli(jax.random.fold_in(key, 12), 0.5, (K,)), 1.0, -1.0)
    weights = jax.random.uniform(jax.random.fold_in(key, 13), (K,), jnp.float32, 0.6, 1.4) * signs
    own_part = jnp.clip(jax.random.normal(jax.random.fold_in(key, 14), (K, N), jnp.float32), -3.0, 3.0) * 0.3
    return (weights[:, None] * shared[None, :] + own_part).astype(jnp.bfloat16)


def draw_matrix(key, part):
    tile_len = 256
    tile_count = N // tile_len

    def one_row(row_tile):

        def one_tile(col_tile):
            lesser = jnp.minimum(row_tile, col_tile)
            greater = jnp.maximum(row_tile, col_tile)
            subkey = jax.random.fold_in(key, lesser * tile_count + greater)
            entries = jax.random.normal(subkey, (tile_len, tile_len), jnp.float32)
            flipped = entries.T
            tile_block = jnp.where(row_tile < col_tile, entries, jnp.where(row_tile > col_tile, flipped, (entries + flipped) * 0.70710678))
            tile_block = tile_block / math.sqrt(N)
            shifts = jax.random.uniform(jax.random.fold_in(key, tile_count * tile_count + row_tile), (tile_len,), jnp.float32, 1.0, 3.0)
            on_diagonal = (row_tile == col_tile).astype(jnp.float32)
            tile_block = tile_block + on_diagonal * jnp.diag(shifts)
            return tile_block
        row_tiles = jax.vmap(one_tile)(jnp.arange(tile_count))
        return jnp.transpose(row_tiles, (1, 0, 2)).reshape(tile_len, N).astype(jnp.bfloat16)
    return lax.map(one_row, jnp.arange(tile_count)).reshape(N, N)


def setup_inputs(seed: int = 0) -> dict:
    key_list = jax.random.split(jax.random.key(seed), 3)
    return {
        "initial": draw_initial(jax.random.fold_in(key_list[2], 71), 0),
        "matrix": draw_matrix(jax.random.fold_in(key_list[2], 71), 0),
    }


def reference(initial, matrix):
    block = initial
    diagonals = []
    updated = jnp.zeros((K, N), jnp.float32)
    for iteration in range(ITERS):
        product = jnp.dot(block.astype(jnp.float32), matrix.astype(jnp.float32), preferred_element_type=jnp.float32)
        gram_matrix = jnp.dot(product, product.T, precision=lax.Precision.HIGHEST)
        factor = jnp.linalg.cholesky(gram_matrix)
        diagonals.append(jnp.diagonal(factor))
        updated = jax.scipy.linalg.solve_triangular(factor, product, lower=True)
        block = updated.astype(jnp.bfloat16)
    return (updated, jnp.stack(diagonals))
```

```python
import functools

import jax
import jax.numpy as jnp
from jax import lax
from jax.experimental import pallas as pl
from jax.experimental.pallas import tpu as pltpu
from jax.sharding import PartitionSpec as P

ITERS = 4
LANES = 128
F32, BF16 = jnp.float32, jnp.bfloat16


def ring_partner(place, shift):
    return place ^ 1 if shift == 0 else 3 - place


def exchange(value, axis, partner):
    pairs = [(i, partner(i)) for i in range(lax.axis_size(axis))]
    return lax.ppermute(value, axis, pairs)


def col_block(value, shift):
    def at(flip_y, flip_x):
        def partner(i):
            y, x = divmod(i, 4)
            y = ring_partner(y, shift) if flip_y else y
            x = ring_partner(x, shift) if flip_x else x
            return y * 4 + x
        return partner
    across = exchange(value, "col", at(True, True))
    along_x = exchange(value, "col", at(False, True))
    along_y = exchange(value, "col", at(True, False))
    return (value, along_x, along_y, across)


def row_block(value):
    def turned(step):
        return lambda i: ((i // 2 + step) % 4) * 2 + i % 2
    far = exchange(value, "row", turned(2))
    up = exchange(value, "row", turned(1))
    down = exchange(value, "row", turned(3))
    return (value, far, up, down)


def total(terms):
    return (terms[0] + terms[1]) + (terms[2] + terms[3])


def sum_over_col(value):
    return col_block(total(col_block(value, 0)), 1)


def sum_over_row(value):
    return row_block(value + exchange(value, "row", lambda i: i ^ 1))


def chunks_of(refs, width):
    return [total([r[:, i:i + LANES] for r in refs]) for i in range(0, width, LANES)]


def whole_row(value, j):
    return jnp.broadcast_to(value[j:j + 1, :], value.shape)


def factored(gram, chunks):
    k = gram.shape[0]
    row = lax.broadcasted_iota(jnp.int32, (k, LANES), 0)
    lane = lax.broadcasted_iota(jnp.int32, (k, LANES), 1)
    columns = [jnp.broadcast_to(gram[:, j:j + 1], (k, LANES)) for j in range(k)]
    diagonal = jnp.zeros((k, LANES), F32)
    for j in range(k):
        pivot = whole_row(columns[j], j)
        inverse = lax.rsqrt(pivot)
        diagonal = jnp.where(lane == j, pivot * inverse, diagonal)
        column = columns[j] * inverse
        for i in range(j + 1, k):
            columns[i] = columns[i] - column * whole_row(column, i)
        below = jnp.where(row > j, column, 0.0)
        here = row == j
        solved = []
        for chunk in chunks:
            line = whole_row(chunk, j) * inverse
            solved.append(jnp.where(here, line, chunk - below * line))
        chunks = solved
    return diagonal, chunks


def store_terms(chunks, terms_ref):
    terms = terms_ref.shape[0] // 8
    for n, chunk in enumerate(chunks):
        parts = []
        for _ in range(terms):
            part = chunk.astype(BF16).astype(F32)
            parts.append(part)
            chunk = chunk - part
        terms_ref[:, n * LANES:(n + 1) * LANES] = jnp.concatenate(parts, 0).astype(BF16)


def rows_added(value):
    out = value[:8]
    for n in range(8, value.shape[0], 8):
        out = out + value[n:n + 8]
    return out


def contract(left, right, right_dim):
    return lax.dot_general(left, right, (((1,), (right_dim,)), ((), ())), preferred_element_type=F32)


def gram_of(terms_ref):
    everything = terms_ref[...]
    gram = None
    for n in range(0, terms_ref.shape[0], 8):
        part = rows_added(contract(everything, terms_ref[n:n + 8, :], 1))
        gram = part if gram is None else gram + part
    return gram


def product_into(out_ref, terms_ref, matrix_ref, right_dim):
    left = terms_ref[...]
    if right_dim == 0:
        out_ref[:, :matrix_ref.shape[1]] = rows_added(contract(left, matrix_ref[...], 0))
    else:
        step = 512
        for n in range(0, matrix_ref.shape[0], step):
            out_ref[:, n:n + step] = rows_added(contract(left, matrix_ref[n:n + step, :], 1))


def first_kernel(block_ref, matrix_ref, out_ref):
    out_ref[...] = contract(block_ref[...], matrix_ref[...], 0)


def step_kernel(normal, right_dim, last, *refs):
    refs = list(refs)
    terms = [refs.pop(0) for _ in range(4)]
    estimates_ref = refs.pop(0) if normal is not None else None
    matrix_ref = None if last else refs.pop(0)
    width = terms[0].shape[1]
    if normal is None:
        out_ref, split_ref = refs
        chunks = chunks_of(terms, width)
    else:
        width -= LANES
        gram = total([t[:, width:] for t in terms])
        if last:
            out_ref, block_ref, estimates_out, split_ref = refs
        else:
            out_ref, estimates_out, split_ref = refs
        diagonal, chunks = factored(gram, chunks_of(terms, width))
        row = lax.broadcasted_iota(jnp.int32, diagonal.shape, 0)
        estimates_out[...] = jnp.where(row == normal, diagonal, estimates_ref[...])
    store_terms(chunks, split_ref)
    gram = gram_of(split_ref)
    if last:
        for n, chunk in enumerate(chunks):
            block_ref[:, n * LANES:(n + 1) * LANES] = chunk
        at = 0
    else:
        product_into(out_ref, split_ref, matrix_ref, right_dim)
        at = out_ref.shape[1] - LANES
    out_ref[:, at:] = jnp.zeros((8, LANES), F32)
    out_ref[:, at:at + 8] = gram


def final_kernel(a_ref, b_ref, c_ref, d_ref, block_ref, estimates_ref, vectors_ref, estimates_out):
    gram = total([r[...] for r in (a_ref, b_ref, c_ref, d_ref)])
    width = block_ref.shape[1]
    chunks = [block_ref[:, n:n + LANES] for n in range(0, width, LANES)]
    diagonal, chunks = factored(gram, chunks)
    for n, chunk in enumerate(chunks):
        vectors_ref[:, n * LANES:(n + 1) * LANES] = chunk
    row = lax.broadcasted_iota(jnp.int32, diagonal.shape, 0)
    everything = jnp.where(row == ITERS - 1, diagonal, estimates_ref[...])
    estimates_out[...] = everything[:ITERS, :8]


def call(kernel, shapes, scratch, name, *args):
    vmem = pl.BlockSpec(memory_space=pltpu.VMEM)
    return pl.pallas_call(
        kernel,
        out_shape=[jax.ShapeDtypeStruct(s, F32) for s in shapes],
        in_specs=[vmem] * len(args),
        out_specs=[vmem] * len(shapes),
        scratch_shapes=[pltpu.VMEM(s, BF16) for s in scratch],
        compiler_params=pltpu.CompilerParams(vmem_limit_bytes=16 << 20),
        name=name,
    )(*args)


def shards(initial, matrix):
    rows, columns = matrix.shape
    k = initial.shape[0]
    matrix = pltpu.with_memory_space_constraint(matrix, pltpu.VMEM)
    copies = jnp.broadcast_to(initial, (lax.axis_size("col"), *initial.shape))
    pieces = lax.all_to_all(copies, "col", split_axis=0, concat_axis=0, tiled=True)
    block = jnp.moveaxis(pieces, 0, 1).reshape(k, rows)

    estimates = jnp.zeros((k, LANES), F32)
    (product,) = call(first_kernel, [(k, columns)], [], "product1", block, matrix)
    terms = sum_over_row(product)
    (product,) = call(
        functools.partial(step_kernel, None, 1, False),
        [(k, rows + LANES)], [(24, columns)], "product2", *terms, matrix)
    terms = sum_over_col(product)
    product, estimates = call(
        functools.partial(step_kernel, 0, 0, False),
        [(k, columns + LANES), (k, LANES)], [(16, rows)], "product3", *terms, estimates, matrix)
    terms = sum_over_row(product)
    product, estimates = call(
        functools.partial(step_kernel, 1, 1, False),
        [(k, rows + LANES), (k, LANES)], [(16, columns)], "product4", *terms, estimates, matrix)
    terms = sum_over_col(product)
    gram, block, estimates = call(
        functools.partial(step_kernel, 2, None, True),
        [(k, LANES), (k, rows), (k, LANES)], [(16, rows)], "last_gram", *terms, estimates)
    terms = sum_over_row(gram)
    own = rows // lax.axis_size("col")
    piece = lax.dynamic_slice_in_dim(block, lax.axis_index("col") * own, own, 1)
    piece = jnp.pad(piece, ((0, 0), (0, -own % LANES)))
    vectors, estimates = call(
        final_kernel, [(k, piece.shape[1]), (ITERS, k)], [], "final", *terms, piece, estimates)
    return (vectors[:, :own], estimates)


def solution(mesh):
    return jax.shard_map(
        shards,
        mesh=mesh,
        in_specs=(P(None, ("row", "col")), P("row", "col")),
        out_specs=(P(None, ("row", "col")), P()),
        check_vma=False,
    )
```

```python
import functools

import jax
import jax.numpy as jnp
from jax import lax
from jax.experimental import pallas as pl
from jax.experimental.pallas import tpu as pltpu
from jax.sharding import PartitionSpec as P

ITERS = 4
LANES = 128
F32, BF16 = jnp.float32, jnp.bfloat16


def ring_partner(place, shift):
    return place ^ 1 if shift == 0 else 3 - place


def exchange(value, axis, partner):
    pairs = [(i, partner(i)) for i in range(lax.axis_size(axis))]
    return lax.ppermute(value, axis, pairs)


def col_block(value, shift):
    def turned(step):
        if shift == 0:
            return lambda i: i // 4 * 4 + (i + step) % 4
        return lambda i: (i + 4 * step) % 16
    far = exchange(value, "col", turned(2))
    up = exchange(value, "col", turned(1))
    down = exchange(value, "col", turned(3))
    return (value, far, up, down)


def row_block(value):
    def turned(step):
        return lambda i: ((i // 2 + step) % 4) * 2 + i % 2
    far = exchange(value, "row", turned(2))
    up = exchange(value, "row", turned(1))
    down = exchange(value, "row", turned(3))
    return (value, far, up, down)


def total(terms):
    return (terms[0] + terms[1]) + (terms[2] + terms[3])


def sum_over_col(value):
    return col_block(total(col_block(value, 0)), 1)


def sum_over_row(value):
    return row_block(value + exchange(value, "row", lambda i: i ^ 1))


def chunks_of(refs, width):
    return [total([r[:, i:i + LANES] for r in refs]) for i in range(0, width, LANES)]


def whole_row(value, j):
    return jnp.broadcast_to(value[j:j + 1, :], value.shape)


def factored(gram, chunks):
    k = gram.shape[0]
    row = lax.broadcasted_iota(jnp.int32, (k, LANES), 0)
    lane = lax.broadcasted_iota(jnp.int32, (k, LANES), 1)
    columns = [jnp.broadcast_to(gram[:, j:j + 1], (k, LANES)) for j in range(k)]
    diagonal = jnp.zeros((k, LANES), F32)
    for j in range(k):
        pivot = whole_row(columns[j], j)
        inverse = lax.rsqrt(pivot)
        diagonal = jnp.where(lane == j, pivot * inverse, diagonal)
        column = columns[j] * inverse
        for i in range(j + 1, k):
            columns[i] = columns[i] - column * whole_row(column, i)
        below = jnp.where(row > j, column, 0.0)
        here = row == j
        solved = []
        for chunk in chunks:
            line = whole_row(chunk, j) * inverse
            solved.append(jnp.where(here, line, chunk - below * line))
        chunks = solved
    return diagonal, chunks


def store_terms(chunks, terms_ref):
    terms = terms_ref.shape[0] // 8
    for n, chunk in enumerate(chunks):
        parts = []
        for _ in range(terms):
            part = chunk.astype(BF16).astype(F32)
            parts.append(part)
            chunk = chunk - part
        terms_ref[:, n * LANES:(n + 1) * LANES] = jnp.concatenate(parts, 0).astype(BF16)


def rows_added(value):
    out = value[:8]
    for n in range(8, value.shape[0], 8):
        out = out + value[n:n + 8]
    return out


def contract(left, right, right_dim):
    return lax.dot_general(left, right, (((1,), (right_dim,)), ((), ())), preferred_element_type=F32)


def gram_of(terms_ref):
    everything = terms_ref[...]
    gram = None
    for n in range(0, terms_ref.shape[0], 8):
        part = rows_added(contract(everything, terms_ref[n:n + 8, :], 1))
        gram = part if gram is None else gram + part
    return gram


def product_into(out_ref, terms_ref, matrix_ref, right_dim):
    left = terms_ref[...]
    if right_dim == 0:
        out_ref[:, :matrix_ref.shape[1]] = rows_added(contract(left, matrix_ref[...], 0))
    else:
        step = 512
        for n in range(0, matrix_ref.shape[0], step):
            out_ref[:, n:n + step] = rows_added(contract(left, matrix_ref[n:n + step, :], 1))


PARTS = 12


def first_kernel(pieces_ref, matrix_ref, out_ref, held_ref, block_ref, arrived):
    size = matrix_ref.shape[0] // PARTS
    own = pieces_ref.shape[2]
    copies = []
    for n in range(PARTS):
        part = pl.ds(n * size, size)
        copies.append(pltpu.make_async_copy(matrix_ref.at[part], held_ref.at[part], arrived.at[n]))
        copies[-1].start()
    for n in range(pieces_ref.shape[0]):
        block_ref[:, n * own:(n + 1) * own] = pieces_ref[n].astype(F32)
    product = None
    for n, copy in enumerate(copies):
        copy.wait()
        part = slice(n * size, (n + 1) * size)
        term = contract(block_ref[:, part].astype(BF16), held_ref[part, :], 0)
        product = term if product is None else product + term
    out_ref[...] = product


def first_product(pieces, matrix):
    pieces_count, k, own = pieces.shape
    vmem = pl.BlockSpec(memory_space=pltpu.VMEM)
    return pl.pallas_call(
        first_kernel,
        out_shape=[
            jax.ShapeDtypeStruct((k, matrix.shape[1]), F32),
            pltpu.VMEM(matrix.shape, matrix.dtype),
        ],
        in_specs=[vmem, pl.BlockSpec(memory_space=pltpu.MemorySpace.HBM)],
        out_specs=[vmem, vmem],
        scratch_shapes=[pltpu.VMEM((k, pieces_count * own), F32), pltpu.SemaphoreType.DMA((PARTS,))],
        compiler_params=pltpu.CompilerParams(vmem_limit_bytes=16 << 20),
        name="product1",
    )(pieces, pltpu.with_memory_space_constraint(matrix, pltpu.MemorySpace.HBM))


def step_kernel(normal, right_dim, last, *refs):
    refs = list(refs)
    terms = [refs.pop(0) for _ in range(4)]
    estimates_ref = refs.pop(0) if normal is not None else None
    matrix_ref = None if last else refs.pop(0)
    width = terms[0].shape[1]
    if normal is None:
        out_ref, split_ref = refs
        chunks = chunks_of(terms, width)
    else:
        width -= LANES
        gram = total([t[:, width:] for t in terms])
        if last:
            out_ref, block_ref, estimates_out, split_ref = refs
        else:
            out_ref, estimates_out, split_ref = refs
        diagonal, chunks = factored(gram, chunks_of(terms, width))
        row = lax.broadcasted_iota(jnp.int32, diagonal.shape, 0)
        estimates_out[...] = jnp.where(row == normal, diagonal, estimates_ref[...])
    store_terms(chunks, split_ref)
    gram = gram_of(split_ref)
    if last:
        for n, chunk in enumerate(chunks):
            block_ref[:, n * LANES:(n + 1) * LANES] = chunk
        at = 0
    else:
        product_into(out_ref, split_ref, matrix_ref, right_dim)
        at = out_ref.shape[1] - LANES
    out_ref[:, at:] = jnp.zeros((8, LANES), F32)
    out_ref[:, at:at + 8] = gram


def final_kernel(a_ref, b_ref, c_ref, d_ref, block_ref, estimates_ref, vectors_ref, estimates_out):
    gram = total([r[...] for r in (a_ref, b_ref, c_ref, d_ref)])
    width = block_ref.shape[1]
    chunks = [block_ref[:, n:n + LANES] for n in range(0, width, LANES)]
    diagonal, chunks = factored(gram, chunks)
    for n, chunk in enumerate(chunks):
        vectors_ref[:, n * LANES:(n + 1) * LANES] = chunk
    row = lax.broadcasted_iota(jnp.int32, diagonal.shape, 0)
    everything = jnp.where(row == ITERS - 1, diagonal, estimates_ref[...])
    estimates_out[...] = everything[:ITERS, :8]


def call(kernel, shapes, scratch, name, *args):
    vmem = pl.BlockSpec(memory_space=pltpu.VMEM)
    return pl.pallas_call(
        kernel,
        out_shape=[jax.ShapeDtypeStruct(s, F32) for s in shapes],
        in_specs=[vmem] * len(args),
        out_specs=[vmem] * len(shapes),
        scratch_shapes=[pltpu.VMEM(s, BF16) for s in scratch],
        compiler_params=pltpu.CompilerParams(vmem_limit_bytes=16 << 20),
        name=name,
    )(*args)


def shards(initial, matrix):
    rows, columns = matrix.shape
    k = initial.shape[0]
    copies = jnp.broadcast_to(initial, (lax.axis_size("col"), *initial.shape))
    pieces = lax.all_to_all(copies, "col", split_axis=0, concat_axis=0, tiled=True)

    estimates = jnp.zeros((k, LANES), F32)
    product, matrix = first_product(pieces, matrix)
    terms = sum_over_row(product)
    (product,) = call(
        functools.partial(step_kernel, None, 1, False),
        [(k, rows + LANES)], [(24, columns)], "product2", *terms, matrix)
    terms = sum_over_col(product)
    product, estimates = call(
        functools.partial(step_kernel, 0, 0, False),
        [(k, columns + LANES), (k, LANES)], [(16, rows)], "product3", *terms, estimates, matrix)
    terms = sum_over_row(product)
    product, estimates = call(
        functools.partial(step_kernel, 1, 1, False),
        [(k, rows + LANES), (k, LANES)], [(16, columns)], "product4", *terms, estimates, matrix)
    terms = sum_over_col(product)
    gram, block, estimates = call(
        functools.partial(step_kernel, 2, None, True),
        [(k, LANES), (k, rows), (k, LANES)], [(16, rows)], "last_gram", *terms, estimates)
    terms = sum_over_row(gram)
    own = rows // lax.axis_size("col")
    piece = lax.dynamic_slice_in_dim(block, lax.axis_index("col") * own, own, 1)
    piece = jnp.pad(piece, ((0, 0), (0, -own % LANES)))
    vectors, estimates = call(
        final_kernel, [(k, piece.shape[1]), (ITERS, k)], [], "final", *terms, piece, estimates)
    return (vectors[:, :own], estimates)


def solution(mesh):
    return jax.shard_map(
        shards,
        mesh=mesh,
        in_specs=(P(None, ("row", "col")), P("row", "col")),
        out_specs=(P(None, ("row", "col")), P()),
        check_vma=False,
    )
```

```python
import functools

import jax
import jax.numpy as jnp
from jax import lax
from jax.experimental import pallas as pl
from jax.experimental.pallas import tpu as pltpu
from jax.sharding import PartitionSpec as P

ITERS = 4
LANES = 128
F32, BF16 = jnp.float32, jnp.bfloat16


def ring_partner(place, shift):
    return place ^ 1 if shift == 0 else 3 - place


def exchange(value, axis, partner):
    pairs = [(i, partner(i)) for i in range(lax.axis_size(axis))]
    return lax.ppermute(value, axis, pairs)


def col_block(value, shift):
    def turned(step):
        if shift == 0:
            return lambda i: i // 4 * 4 + (i + step) % 4
        return lambda i: (i + 4 * step) % 16
    far = exchange(value, "col", turned(2))
    up = exchange(value, "col", turned(1))
    down = exchange(value, "col", turned(3))
    return (value, far, up, down)


def row_block(value):
    def turned(step):
        return lambda i: ((i // 2 + step) % 4) * 2 + i % 2
    far = exchange(value, "row", turned(2))
    up = exchange(value, "row", turned(1))
    down = exchange(value, "row", turned(3))
    return (value, far, up, down)


def total(terms):
    return (terms[0] + terms[1]) + (terms[2] + terms[3])


def sum_over_col(value):
    return col_block(total(col_block(value, 0)), 1)


def sum_over_row(value):
    return row_block(value + exchange(value, "row", lambda i: i ^ 1))


def gathered_over_col(value, held):
    def turned(step_y, step_x):
        return lambda i: (i // 4 - step_y) % 4 * 4 + (i % 4 - step_x) % 4
    far, up, down = (exchange(value, "col", turned(0, n)) for n in (2, 1, 3))
    vmem = pl.BlockSpec(memory_space=pltpu.VMEM)
    line = pl.pallas_call(
        line_kernel,
        out_shape=jax.ShapeDtypeStruct((4, *value.shape), value.dtype),
        in_specs=[vmem] * 5,
        out_specs=vmem,
        compiler_params=pltpu.CompilerParams(vmem_limit_bytes=1 << 20),
        name="line",
    )(value, far, up, down, held)
    far, up, down = (exchange(line, "col", turned(n, 0)) for n in (2, 1, 3))
    return (line, far, up, down)


def chunks_of(refs, width):
    return [total([r[:, i:i + LANES] for r in refs]) for i in range(0, width, LANES)]


def whole_row(value, j):
    return jnp.broadcast_to(value[j:j + 1, :], value.shape)


def factored(gram, chunks):
    k = gram.shape[0]
    row = lax.broadcasted_iota(jnp.int32, (k, LANES), 0)
    lane = lax.broadcasted_iota(jnp.int32, (k, LANES), 1)
    columns = [jnp.broadcast_to(gram[:, j:j + 1], (k, LANES)) for j in range(k)]
    diagonal = jnp.zeros((k, LANES), F32)
    for j in range(k):
        pivot = whole_row(columns[j], j)
        inverse = lax.rsqrt(pivot)
        diagonal = jnp.where(lane == j, pivot * inverse, diagonal)
        column = columns[j] * inverse
        for i in range(j + 1, k):
            columns[i] = columns[i] - column * whole_row(column, i)
        below = jnp.where(row > j, column, 0.0)
        here = row == j
        solved = []
        for chunk in chunks:
            line = whole_row(chunk, j) * inverse
            solved.append(jnp.where(here, line, chunk - below * line))
        chunks = solved
    return diagonal, chunks


def store_terms(chunks, terms_ref):
    terms = terms_ref.shape[0] // 8
    for n, chunk in enumerate(chunks):
        parts = []
        for _ in range(terms):
            part = chunk.astype(BF16).astype(F32)
            parts.append(part)
            chunk = chunk - part
        terms_ref[:, n * LANES:(n + 1) * LANES] = jnp.concatenate(parts, 0).astype(BF16)


def rows_added(value):
    out = value[:8]
    for n in range(8, value.shape[0], 8):
        out = out + value[n:n + 8]
    return out


def contract(left, right, right_dim):
    return lax.dot_general(left, right, (((1,), (right_dim,)), ((), ())), preferred_element_type=F32)


def gram_of(terms_ref):
    everything = terms_ref[...]
    gram = None
    for n in range(0, terms_ref.shape[0], 8):
        part = rows_added(contract(everything, terms_ref[n:n + 8, :], 1))
        gram = part if gram is None else gram + part
    return gram


def contract_rows(left, matrix_refs):
    out, at = None, 0
    for ref in matrix_refs:
        part = contract(left[:, at:at + ref.shape[0]], ref[...], 0)
        out = part if out is None else out + part
        at += ref.shape[0]
    return out


def product_into(out_ref, terms_ref, matrix_refs, right_dim):
    left = terms_ref[...]
    if right_dim == 0:
        out_ref[:, :matrix_refs[0].shape[1]] = rows_added(contract_rows(left, matrix_refs))
        return
    step, at = 512, 0
    for ref in matrix_refs:
        for n in range(0, ref.shape[0], step):
            out_ref[:, at:at + step] = rows_added(contract(left, ref[n:n + step, :], 1))
            at += step


def line_kernel(a_ref, c_ref, b_ref, d_ref, held_ref, line_ref):
    del held_ref
    for n, ref in enumerate((a_ref, b_ref, c_ref, d_ref)):
        line_ref[n] = ref[...]


def first_kernel(a_ref, c_ref, b_ref, d_ref, *refs):
    *matrix_refs, out_ref, block_ref = refs
    own = a_ref.shape[2]
    place = lax.axis_index("col")
    for mine in range(16):
        @pl.when(place == mine)
        def _():
            for b, ref in enumerate((a_ref, b_ref, c_ref, d_ref)):
                for a in range(4):
                    n = (mine // 4 + b) % 4 * 4 + (mine % 4 + a) % 4
                    block_ref[:, n * own:(n + 1) * own] = ref[a].astype(F32)
    out_ref[...] = contract_rows(block_ref[...].astype(BF16), matrix_refs)


PARTS = 6


def load_kernel(start, matrix_ref, held_ref, arrived):
    size = held_ref.shape[0] // PARTS
    copies = []
    for n in range(PARTS):
        source = matrix_ref.at[pl.ds(start + n * size, size)]
        copies.append(pltpu.make_async_copy(source, held_ref.at[pl.ds(n * size, size)], arrived.at[n]))
        copies[-1].start()
    for copy in copies:
        copy.wait()


def held_half(matrix, half):
    rows, columns = matrix.shape
    return pl.pallas_call(
        functools.partial(load_kernel, half * (rows // 2)),
        out_shape=pltpu.VMEM((rows // 2, columns), matrix.dtype),
        in_specs=[pl.BlockSpec(memory_space=pltpu.MemorySpace.HBM)],
        out_specs=pl.BlockSpec(memory_space=pltpu.VMEM),
        scratch_shapes=[pltpu.SemaphoreType.DMA((PARTS,))],
        cost_estimate=pl.CostEstimate(flops=0, bytes_accessed=matrix.size, transcendentals=0),
        compiler_params=pltpu.CompilerParams(vmem_limit_bytes=16 << 20),
        name=f"held_half{half}",
    )(matrix)


def step_kernel(normal, right_dim, last, *refs):
    refs = list(refs)
    terms = [refs.pop(0) for _ in range(4)]
    estimates_ref = refs.pop(0) if normal is not None else None
    matrix_refs = None if last else [refs.pop(0) for _ in range(2)]
    width = terms[0].shape[1]
    if normal is None:
        out_ref, split_ref = refs
        chunks = chunks_of(terms, width)
    else:
        width -= LANES
        gram = total([t[:, width:] for t in terms])
        if last:
            out_ref, block_ref, estimates_out, split_ref = refs
        else:
            out_ref, estimates_out, split_ref = refs
        diagonal, chunks = factored(gram, chunks_of(terms, width))
        row = lax.broadcasted_iota(jnp.int32, diagonal.shape, 0)
        estimates_out[...] = jnp.where(row == normal, diagonal, estimates_ref[...])
    store_terms(chunks, split_ref)
    gram = gram_of(split_ref)
    if last:
        for n, chunk in enumerate(chunks):
            block_ref[:, n * LANES:(n + 1) * LANES] = chunk
        at = 0
    else:
        product_into(out_ref, split_ref, matrix_refs, right_dim)
        at = out_ref.shape[1] - LANES
    out_ref[:, at:] = jnp.zeros((8, LANES), F32)
    out_ref[:, at:at + 8] = gram


def final_kernel(a_ref, b_ref, c_ref, d_ref, block_ref, estimates_ref, vectors_ref, estimates_out):
    gram = total([r[...] for r in (a_ref, b_ref, c_ref, d_ref)])
    width = block_ref.shape[1]
    chunks = [block_ref[:, n:n + LANES] for n in range(0, width, LANES)]
    diagonal, chunks = factored(gram, chunks)
    for n, chunk in enumerate(chunks):
        vectors_ref[:, n * LANES:(n + 1) * LANES] = chunk
    row = lax.broadcasted_iota(jnp.int32, diagonal.shape, 0)
    everything = jnp.where(row == ITERS - 1, diagonal, estimates_ref[...])
    estimates_out[...] = everything[:ITERS, :8]


def call(kernel, shapes, scratch, name, *args):
    vmem = pl.BlockSpec(memory_space=pltpu.VMEM)
    return pl.pallas_call(
        kernel,
        out_shape=[jax.ShapeDtypeStruct(s, F32) for s in shapes],
        in_specs=[vmem] * len(args),
        out_specs=[vmem] * len(shapes),
        scratch_shapes=[pltpu.VMEM(s, t) for s, t in scratch],
        compiler_params=pltpu.CompilerParams(vmem_limit_bytes=16 << 20),
        name=name,
    )(*args)


def shards(initial, matrix):
    rows, columns = matrix.shape
    k = initial.shape[0]
    matrix = pltpu.with_memory_space_constraint(matrix, pltpu.MemorySpace.HBM)
    halves = [held_half(matrix, n) for n in range(2)]
    pieces = gathered_over_col(initial, halves[0])

    estimates = jnp.zeros((k, LANES), F32)
    (product,) = call(
        first_kernel, [(k, columns)], [((k, rows), F32)], "product1", *pieces, *halves)
    terms = sum_over_row(product)
    (product,) = call(
        functools.partial(step_kernel, None, 1, False),
        [(k, rows + LANES)], [((24, columns), BF16)], "product2", *terms, *halves)
    terms = sum_over_col(product)
    product, estimates = call(
        functools.partial(step_kernel, 0, 0, False),
        [(k, columns + LANES), (k, LANES)], [((16, rows), BF16)], "product3", *terms, estimates, *halves)
    terms = sum_over_row(product)
    product, estimates = call(
        functools.partial(step_kernel, 1, 1, False),
        [(k, rows + LANES), (k, LANES)], [((16, columns), BF16)], "product4", *terms, estimates, *halves)
    terms = sum_over_col(product)
    gram, block, estimates = call(
        functools.partial(step_kernel, 2, None, True),
        [(k, LANES), (k, rows), (k, LANES)], [((16, rows), BF16)], "last_gram", *terms, estimates)
    terms = sum_over_row(gram)
    own = rows // lax.axis_size("col")
    piece = lax.dynamic_slice_in_dim(block, lax.axis_index("col") * own, own, 1)
    piece = jnp.pad(piece, ((0, 0), (0, -own % LANES)))
    vectors, estimates = call(
        final_kernel, [(k, piece.shape[1]), (ITERS, k)], [], "final", *terms, piece, estimates)
    return (vectors[:, :own], estimates)


def solution(mesh):
    return jax.shard_map(
        shards,
        mesh=mesh,
        in_specs=(P(None, ("row", "col")), P("row", "col")),
        out_specs=(P(None, ("row", "col")), P()),
        check_vma=False,
    )
```
